32 devices in a mesh: shard: 4 (over x, core), ctx: 8 (over z, y).
Axes of the slice: x: 2, y: 2, z: 4, core: 2. Of those that a mesh axis runs over, the one named last changes fastest.
Arguments:
- tokens: bfloat16 [2, 2048, 768], P(None, ('ctx', 'shard')), may hold values from -6 to 6
- gain_attn: float32 [768], replicated, may hold values from 0.5 to 1.5
- gain_ffn: float32 [768], replicated, may hold values from 0.5 to 1.5
- query_key_value_weight: bfloat16 [768, 2304], P('shard'), may hold values from -0.21875 to 0.21875
- attention_out_weight: bfloat16 [768, 768], P('shard'), may hold values from -6 to 6
- feedforward_in_weight: bfloat16 [768, 2304], P('shard'), may hold values from -0.21875 to 0.21875
- feedforward_out_weight: bfloat16 [1152, 768], P('shard'), may hold values from -0.1875 to 0.1875
- cotangent: bfloat16 [2, 2048, 768], P(None, ('ctx', 'shard')), may hold values from -6 to 6
Outputs:
- output: bfloat16 [2, 2048, 768], P(None, ('ctx', 'shard'))
- grad_tokens: bfloat16 [2, 2048, 768], P(None, ('ctx', 'shard'))
- grad_gain_attn: float32 [768], replicated
- grad_gain_ffn: float32 [768], replicated
- grad_w_qkv: float32 [768, 2304], P('shard')
- grad_w_attn: float32 [768, 768], P('shard')
- grad_w_in: float32 [768, 2304], P('shard')
- grad_w_out: float32 [1152, 768], P('shard')
The draws below stay inside these ranges and needn't reach their ends.
All inputs are finite; a program needn't handle non-finite values.
Results may differ from the reference program's by a relative error of at most 0.02.
Values may be sent and summed in bfloat16 or wider, within the bound.
No kernel may reach another device: no remote copies, remote signals or barrier semaphores. Data moves between devices by JAX's collectives and lax.ppermute only.
A program may use at most 192 MiB of HBM per device.

```python
import jax
import jax.numpy as jnp
from jax import lax

D = 768
HEADS = 12
HEAD_DIM = 64
FF = 1152
SEQS = 2
SEQLEN = 2048


def level_of(stream_key, dims, shards, least, top_value):
    loudness = 1.0
    for axis_at, shards_of in shards:
        heights = jax.random.uniform(jax.random.fold_in(jax.random.fold_in(stream_key, 6), axis_at), (shards_of,), jnp.float32, least / len(shards), top_value / len(shards))
        loudness = loudness * jnp.repeat(jnp.exp(heights), dims[axis_at] // shards_of).reshape((-1,) + (1,) * (len(dims) - 1 - axis_at))
    return loudness


def centred(own_key, shape, scale, most, cuts=(), held_as=jnp.bfloat16):
    drawn = scale * jax.random.normal(own_key, shape, jnp.float32)
    if cuts:
        drawn = drawn * level_of(own_key, shape, cuts, -0.22, 0.18)
    return jnp.clip(drawn, -most, most).astype(held_as)


def setup_inputs(seed: int = 0) -> dict:
    seeds = jax.random.split(jax.random.key(seed), 9)
    tokens = centred(seeds[0], (SEQS, SEQLEN, D), 1.0, 6.0, ((1, 32),))
    gain_attn = jnp.clip(1.0 + 0.1 * jax.random.normal(seeds[1], (D,), jnp.float32), 0.5, 1.5)
    gain_ffn = jnp.clip(1.0 + 0.1 * jax.random.normal(seeds[2], (D,), jnp.float32), 0.5, 1.5)
    query_key_value_weight = centred(seeds[3], (D, 3 * D), D ** -0.5, 0.21875, ((0, 4),))
    attention_out_weight = centred(seeds[4], (D, D), (max(1, SEQLEN // 2048) ** 0.5), 6.0, ((0, 4),))
    feedforward_in_weight = centred(seeds[5], (D, 2 * FF), D ** -0.5, 0.21875, ((0, 4),))
    feedforward_out_weight = centred(seeds[6], (FF, D), FF ** -0.5, 0.1875, ((0, 4),))
    cotangent = centred(seeds[7], (SEQS, SEQLEN, D), 1.0, 6.0, ((1, 32),))
    return {"tokens": tokens, "gain_attn": gain_attn, "gain_ffn": gain_ffn, "query_key_value_weight": query_key_value_weight, "attention_out_weight": attention_out_weight, "feedforward_in_weight": feedforward_in_weight, "feedforward_out_weight": feedforward_out_weight, "cotangent": cotangent}


@jax.custom_vjp
def low(v):
    return lax.optimization_barrier(v.astype(jnp.bfloat16)).astype(jnp.float32)

@jax.custom_vjp
def lowered_backward(v):
    return v

def low_keep(v):
    return (low(v), None)

def low_pass(kept, grad):
    return (grad,)

def back_keep(v):
    return (v, None)

def back_low(kept, grad):
    return (low(grad),)
low.defvjp(low_keep, low_pass)
lowered_backward.defvjp(back_keep, back_low)
epsilon = 1e-05
rope_base = 160000.0
highest_precision = lax.Precision.HIGHEST

def layer_norm(values, scale_vector):
    centre = lax.optimization_barrier(jnp.mean(values, axis=-1, keepdims=True))
    shifted = values - centre
    spread = lax.optimization_barrier(jnp.mean(shifted * shifted, axis=-1, keepdims=True))
    return shifted * lax.rsqrt(spread + epsilon) * scale_vector

def rope_tables(positions, half_dim):
    freq_index = jnp.arange(half_dim, dtype=jnp.float32)
    inverse_freq = jnp.exp(freq_index * (-1.0 / half_dim) * jnp.log(jnp.float32(rope_base)))
    angles = positions[:, None] * inverse_freq[None, :]
    angles = jnp.concatenate([angles, angles], axis=1)
    return (jnp.cos(angles), jnp.sin(angles))

def rotate(values, cosine, sine_table, half_dim):
    turned = jnp.concatenate([-values[..., half_dim:], values[..., :half_dim]], axis=-1)
    return values * cosine[:, None, :] + turned * sine_table[:, None, :]

def attend_rows(query_block, key_rows, value_rows):
    scores = jnp.einsum('qhd,khd->hqk', query_block, key_rows, precision=highest_precision) * HEAD_DIM ** (-0.5)
    scores = lowered_backward(scores)
    row_max = lax.optimization_barrier(jnp.max(scores, axis=-1, keepdims=True))
    weights = jnp.exp(scores - row_max)
    probabilities = low(weights / lax.optimization_barrier(jnp.sum(weights, axis=-1, keepdims=True)))
    return jnp.einsum('hqk,khd->qhd', probabilities, value_rows, precision=highest_precision)

def attend_sequence(packed):
    queries, key_rows, value_rows = packed
    block_rows = min(512, SEQLEN)
    blocks = SEQLEN // block_rows
    query_blocks = queries.reshape(blocks, block_rows, HEADS, HEAD_DIM)
    block_fn = jax.checkpoint(lambda query_block: attend_rows(query_block, key_rows, value_rows))
    return lax.map(block_fn, query_blocks).reshape(SEQLEN, HEADS, HEAD_DIM)

def block_forward(layer_input, gain_attn, gain_ffn, query_key_value_weight, attention_out_weight, feedforward_in_weight, feedforward_out_weight):
    half_dim = HEAD_DIM // 2
    attention_normed = low(layer_norm(layer_input, gain_attn))
    query_key_value_rows = lowered_backward(jnp.einsum('mxc,cn->mxn', attention_normed, query_key_value_weight, precision=highest_precision))
    query_key_value_rows = query_key_value_rows.reshape(SEQS, SEQLEN, 3, HEADS, HEAD_DIM)
    cosine, sine_table = rope_tables(jnp.arange(SEQLEN, dtype=jnp.float32), half_dim)
    queries = low(rotate(query_key_value_rows[:, :, 0], cosine, sine_table, half_dim))
    key_rows = low(rotate(query_key_value_rows[:, :, 1], cosine, sine_table, half_dim))
    value_rows = low(query_key_value_rows[:, :, 2])
    attention_result = lax.map(attend_sequence, (queries, key_rows, value_rows)).reshape(SEQS, SEQLEN, D)
    attention_result = low(lowered_backward(attention_result))
    residual_middle = layer_input + lowered_backward(jnp.einsum('mxc,cn->mxn', attention_result, attention_out_weight, precision=highest_precision))
    feedforward_normed = low(layer_norm(residual_middle, gain_ffn))
    gate_up_values = lowered_backward(jnp.einsum('mxc,cn->mxn', feedforward_normed, feedforward_in_weight, precision=highest_precision))
    hidden_activation = low(jax.nn.gelu(gate_up_values[..., :FF], approximate=False) * gate_up_values[..., FF:])
    return residual_middle + jnp.einsum('yrz,zb->yrb', hidden_activation, feedforward_out_weight, precision=highest_precision)

def reference(tokens, gain_attn, gain_ffn, query_key_value_weight, attention_out_weight, feedforward_in_weight, feedforward_out_weight, cotangent):
    result, pullback = jax.vjp(block_forward, tokens.astype(jnp.float32), gain_attn, gain_ffn, query_key_value_weight.astype(jnp.float32), attention_out_weight.astype(jnp.float32), feedforward_in_weight.astype(jnp.float32), feedforward_out_weight.astype(jnp.float32))
    grads = pullback(cotangent.astype(jnp.float32))
    return (result.astype(jnp.bfloat16), grads[0].astype(jnp.bfloat16), grads[1], grads[2], grads[3], grads[4], grads[5], grads[6])
```

```python
import functools

import jax
import jax.numpy as jnp
from jax import lax
from jax.experimental import pallas as pl
from jax.experimental.pallas import tpu as pltpu
from jax.sharding import Mesh, PartitionSpec as P

HEADS = 12
HEAD_DIM = 64
HALF = HEAD_DIM // 2
SCALE = HEAD_DIM ** (-0.5)

epsilon = 1e-05
rope_base = 160000.0
f32 = jnp.float32
bf16 = jnp.bfloat16
VMEM_LIMIT = 56 * 2**20


def low(v):
    return v.astype(bf16)


def swap(v, axis):
    return lax.ppermute(v, axis, [(0, 1), (1, 0)])


def swap_z(v, bit):
    count = lax.axis_size("z")
    return lax.ppermute(v, "z", [(i, i ^ bit) for i in range(count)])


def across(v):
    return lax.ppermute(v, ("x", "core"), [(i, 3 - i) for i in range(4)])


def z_bits():
    bits, bit = [], 1
    while bit < lax.axis_size("z"):
        bits.append(bit)
        bit *= 2
    return bits


def z_offsets():
    offsets = [0]
    for bit in reversed(z_bits()):
        offsets = offsets + [o ^ bit for o in offsets]
    return offsets


SLOT_SHARD = [2 * (e & 1) + (e >> 1) for e in range(4)]


def gather_shard(v):
    from_x = swap(v, "x")
    from_core = swap(v, "core")
    return [v, from_x, from_core, swap(from_x, "core")]


def exchange_shard(parts):
    return [parts[0], swap(parts[1], "x"), swap(parts[2], "core"), across(parts[3])]


def pick(v, index):
    return lax.dynamic_index_in_dim(v, index, 0, keepdims=False)


def pair_in_order(own, other, bit):
    return jnp.where(bit == 0, jnp.stack([own, other]), jnp.stack([other, own]))


def ctx_sum(value, z_index, y_index):
    rest = value.shape[1:]
    value = value.reshape((2, -1) + rest)
    value = pick(value, y_index) + swap(low(pick(value, 1 - y_index)), "y").astype(f32)
    for bit in z_bits():
        mine = (z_index // bit) % 2
        value = value.reshape((2, -1) + rest)
        value = pick(value, mine) + swap_z(low(pick(value, 1 - mine)), bit).astype(f32)
    return value.reshape(rest)


def ctx_gather(value, z_index, y_index):
    rest = value.shape
    value = value[None]
    for bit in reversed(z_bits()):
        value = pair_in_order(value, swap_z(value, bit), (z_index // bit) % 2)
        value = value.reshape((-1,) + rest)
    value = pair_in_order(value, swap(value, "y"), y_index)
    return value.reshape((-1,) + rest)


def norm_parts(values):
    centre = jnp.mean(values, axis=-1, keepdims=True)
    shifted = values - centre
    spread = jnp.mean(shifted * shifted, axis=-1, keepdims=True)
    inv = lax.rsqrt(spread + epsilon)
    return shifted * inv, inv


def norm_back(grad_normed, gain, xhat, inv):
    e = grad_normed * gain
    return inv * (
        e
        - jnp.mean(e, axis=-1, keepdims=True)
        - xhat * jnp.mean(e * xhat, axis=-1, keepdims=True)
    )


def dot(a, b):
    return jnp.dot(a, b, preferred_element_type=f32)


def dot_nt(a, b):
    return lax.dot_general(a, b, (((1,), (1,)), ((), ())), preferred_element_type=f32)


def dot_tn(a, b):
    return lax.dot_general(a, b, (((0,), (0,)), ((), ())), preferred_element_type=f32)


def phi_parts(gate):
    cdf = 0.5 * (1.0 + lax.erf(gate * (0.5**0.5)))
    pdf = jnp.exp(-0.5 * gate * gate) * 0.3989422804014327
    return cdf, pdf


def turn(u, tables, sign):
    cosine, sine_low, sine_high = tables
    turned = pltpu.roll(u, 96, 1) * sine_low + pltpu.roll(u, 32, 1) * sine_high
    return u * cosine + sign * turned


def make_tables(base_cos, base_sin, row_cos, row_sin):
    cosine = base_cos * row_cos - base_sin * row_sin
    sine = base_sin * row_cos + base_cos * row_sin
    is_low = lax.broadcasted_iota(jnp.int32, sine.shape, 1) % HEAD_DIM < HALF
    return cosine, jnp.where(is_low, -sine, 0.0), jnp.where(is_low, 0.0, sine)


def turn_mixed(u, tables, sign):
    is_key = lax.broadcasted_iota(jnp.int32, u.shape, 1) < HEAD_DIM
    return jnp.where(is_key, turn(u, tables, sign), u)


def in_row_order(index_ref, parts, scratch):
    rows = parts[0].shape[0]
    for e, part in enumerate(parts):
        at = pl.multiple_of((index_ref[0] ^ SLOT_SHARD[e]) * rows, rows)
        scratch[pl.ds(at, rows), :] = part[...]


def params():
    return pltpu.CompilerParams(vmem_limit_bytes=VMEM_LIMIT)


IN_SMEM = pl.BlockSpec(memory_space=pltpu.SMEM)
IN_VMEM = pl.BlockSpec(memory_space=pltpu.VMEM)


def prepare_kernel(index_ref, qkv_ref, in_ref, *outs):
    shard = index_ref[0]
    width = qkv_ref.shape[1] // 12
    ff = in_ref.shape[1] // 8
    for s in range(4):

        @pl.when(shard == s)
        def _():
            for e in range(4):
                t = s ^ SLOT_SHARD[e]
                for place, third in enumerate((1, 2, 0)):
                    at = third * 4 * width + t * width
                    outs[e][:, place * width : (place + 1) * width] = qkv_ref[:, at : at + width]
                for half in range(2):
                    at = half * 4 * ff + t * ff
                    outs[4 + e][:, half * ff : (half + 1) * ff] = in_ref[:, at : at + ff]


def prepare(index, w_qkv, w_in):
    rows = w_qkv.shape[0]
    shapes = [jax.ShapeDtypeStruct((rows, w_qkv.shape[1] // 4), bf16)] * 4
    shapes += [jax.ShapeDtypeStruct((rows, w_in.shape[1] // 4), bf16)] * 4
    whole = pl.BlockSpec(memory_space=pltpu.VMEM)
    got = pl.pallas_call(
        prepare_kernel,
        out_shape=shapes,
        in_specs=[pl.BlockSpec(memory_space=pltpu.SMEM), whole, whole],
        out_specs=[whole] * 8,
        compiler_params=pltpu.CompilerParams(vmem_limit_bytes=VMEM_LIMIT),
        name="prepare",
    )(index, w_qkv, w_in)
    return got[:4], got[4:]


def attend_kernel(q_ref, kv_ref, attn_ref, low_ref, lse_ref, max_ref, sum_ref, acc_ref):
    at = pl.program_id(0)
    heads = q_ref.shape[1] // HEAD_DIM
    width = heads * HEAD_DIM

    @pl.when(at == 0)
    def _():
        max_ref[...] = jnp.full(max_ref.shape, -1e30, f32)
        sum_ref[...] = jnp.zeros(sum_ref.shape, f32)
        acc_ref[...] = jnp.zeros(acc_ref.shape, f32)

    block = min(256, q_ref.shape[0])
    for h in range(heads):
        cols = slice(h * HEAD_DIM, (h + 1) * HEAD_DIM)
        key = kv_ref[:, cols]
        value = kv_ref[:, width + h * HEAD_DIM : width + (h + 1) * HEAD_DIM]
        for start in range(0, q_ref.shape[0], block):
            rows = slice(start, start + block)
            scores = dot_nt(q_ref[rows, cols], key)
            old = max_ref[rows, h : h + 1]
            new = jnp.maximum(old, jnp.max(scores, axis=1, keepdims=True))
            weights = jnp.exp(scores - new)
            factor = jnp.exp(old - new)
            max_ref[rows, h : h + 1] = new
            total = sum_ref[rows, h : h + 1] * factor + jnp.sum(weights, axis=1, keepdims=True)
            sum_ref[rows, h : h + 1] = total
            acc = acc_ref[rows, cols] * factor + dot(low(weights), value)
            acc_ref[rows, cols] = acc

    @pl.when(at == pl.num_programs(0) - 1)
    def _():
        for h in range(heads):
            cols = slice(h * HEAD_DIM, (h + 1) * HEAD_DIM)
            attn = acc_ref[:, cols] / sum_ref[:, h : h + 1]
            attn_ref[:, cols] = attn
            low_ref[:, cols] = low(attn)
            lse_ref[:, h : h + 1] = max_ref[:, h : h + 1] + jnp.log(sum_ref[:, h : h + 1])


def attend(query, kv):
    rows, width = query.shape
    chunk = min(2048, kv.shape[0])
    fixed = lambda shape: pl.BlockSpec(shape, lambda i: (0, 0))
    return pl.pallas_call(
        attend_kernel,
        grid=(kv.shape[0] // chunk,),
        in_specs=[fixed((rows, width)), pl.BlockSpec((chunk, 2 * width), lambda i: (i, 0))],
        out_specs=[fixed((rows, width)), fixed((rows, width)), fixed((rows, 128))],
        out_shape=[
            jax.ShapeDtypeStruct((rows, width), f32),
            jax.ShapeDtypeStruct((rows, width), bf16),
            jax.ShapeDtypeStruct((rows, 128), f32),
        ],
        scratch_shapes=[
            pltpu.VMEM((rows, 128), f32),
            pltpu.VMEM((rows, 128), f32),
            pltpu.VMEM((rows, width), f32),
        ],
        compiler_params=pltpu.CompilerParams(vmem_limit_bytes=VMEM_LIMIT),
        name="attend",
    )(query, kv)


def attend_back_kernel(
    q_ref, kv_ref, half_ref, other_ref, w_ref, attn_ref, lse_ref,
    base_cos, base_sin, q_base_cos, q_base_sin, row_cos, row_sin,
    dkv_ref, dq_ref, dq_scr, dkv_scr, lse_scr, delta_scr, grad_scr,
):
    at = pl.program_id(0)
    width = q_ref.shape[1]
    heads = width // HEAD_DIM
    keys = kv_ref.shape[0]
    block = min(512, keys)
    segment = row_cos.shape[0]

    @pl.when(at == 0)
    def _():
        half = half_ref.shape[0]
        grad_scr[:half, :] = low(dot_nt(half_ref[...], w_ref[...]))
        grad_scr[half:, :] = low(dot_nt(other_ref[...], w_ref[...]))
        dq_scr[...] = jnp.zeros(dq_scr.shape, f32)
        lse_scr[...] = lse_ref[...].T
        for h in range(heads):
            cols = slice(h * HEAD_DIM, (h + 1) * HEAD_DIM)
            both = (grad_scr[:, cols].astype(f32) * attn_ref[:, cols]).T
            delta_scr[h : h + 1, :] = jnp.sum(both, axis=0, keepdims=True)

    for h in range(heads):
        cols = slice(h * HEAD_DIM, (h + 1) * HEAD_DIM)
        vcols = slice(width + h * HEAD_DIM, width + (h + 1) * HEAD_DIM)
        query, grad = q_ref[:, cols], grad_scr[:, cols]
        lse, delta = lse_scr[h : h + 1, :], delta_scr[h : h + 1, :]

        def step(i, carry):
            rows = pl.ds(i * block, block)
            key, value = kv_ref[rows, cols], kv_ref[rows, vcols]
            probs = jnp.exp(dot_nt(key, query) - lse)
            dkv_scr[rows, vcols] = dot(low(probs), grad)
            grad_scores = low(probs * (dot_nt(value, grad) - delta))
            dkv_scr[rows, cols] = dot(grad_scores, query)
            dq_scr[cols, :] += dot_tn(key, grad_scores)
            return carry

        lax.fori_loop(0, keys // block, step, 0)

    def finish(i, carry):
        rows = pl.ds(i * segment, segment)
        one = pl.ds(i, 1)
        tables = make_tables(base_cos[one, :], base_sin[one, :], row_cos[...], row_sin[...])
        dkv_ref[rows, :128] = low(turn(dkv_scr[rows, :128], tables, -1.0))
        dkv_ref[rows, 128:256] = low(turn_mixed(dkv_scr[rows, 128:256], tables, -1.0))
        dkv_ref[rows, 256:] = low(dkv_scr[rows, 256:])
        return carry

    lax.fori_loop(0, keys // segment, finish, 0)

    @pl.when(at == pl.num_programs(0) - 1)
    def _():
        first = dq_scr[:128, :].T * SCALE
        second = dq_scr[128:, :].T * SCALE
        for g in range(q_base_cos.shape[0]):
            rows = slice(g * segment, (g + 1) * segment)
            tables = make_tables(
                q_base_cos[g : g + 1, :], q_base_sin[g : g + 1, :], row_cos[...], row_sin[...]
            )
            dq_ref[rows, :128] = low(turn(first[rows], tables, -1.0))
            dq_ref[rows, 128:] = low(turn(second[rows], tables, -1.0)[:, : width - 128])


def attend_back(query, kv, half, other, w_attn, attn, lse, bases, q_bases, row_tables):
    rows, width = query.shape
    chunk = min(2048, kv.shape[0])
    segments = chunk // row_tables[0].shape[0]
    fixed = lambda v: pl.BlockSpec(v.shape, lambda i: (0, 0))
    moving = lambda n, cols: pl.BlockSpec((n, cols), lambda i: (i, 0))
    still = (half, other, w_attn, attn, lse)
    return pl.pallas_call(
        attend_back_kernel,
        grid=(kv.shape[0] // chunk,),
        in_specs=[fixed(query), moving(chunk, 2 * width)]
        + [fixed(v) for v in still]
        + [moving(segments, 128)] * 2
        + [fixed(v) for v in q_bases + row_tables],
        out_specs=[moving(chunk, 2 * width), pl.BlockSpec((rows, width), lambda i: (0, 0))],
        out_shape=[
            jax.ShapeDtypeStruct(kv.shape, bf16),
            jax.ShapeDtypeStruct((rows, width), bf16),
        ],
        scratch_shapes=[
            pltpu.VMEM((256, rows), f32),
            pltpu.VMEM((chunk, 2 * width), f32),
            pltpu.VMEM((128, rows), f32),
            pltpu.VMEM((8, rows), f32),
            pltpu.VMEM((rows, width), bf16),
        ],
        compiler_params=params(),
        name="attend_back",
    )(query, kv, *still, *bases, *q_bases, *row_tables)


def project_kernel(
    index_ref, a_ref, b_ref, base_cos, base_sin, row_cos, row_sin, gain_ref, w0, w1, w2, w3,
    normed_ref, kv_ref, q_ref, w_scr,
):
    width = q_ref.shape[2]
    segment = row_cos.shape[0]

    @pl.when(pl.program_id(0) == 0)
    def _():
        in_row_order(index_ref, (w0, w1, w2, w3), w_scr)

    tokens = a_ref.shape[1]
    block = min(256, tokens)
    w_kv, w_q = w_scr[:, : 2 * width], w_scr[:, 2 * width :]
    for dy, ref in enumerate((a_ref, b_ref)):
        for start in range(0, tokens, block):
            here = slice(start, start + block)
            xhat, _ = norm_parts(ref[0, here, :].astype(f32))
            normed = low(xhat * gain_ref[...])
            normed_ref[0, dy, here, :] = normed
            kv = dot(normed, w_kv)
            for at in range(0, block, segment):
                g = dy * (tokens // segment) + (start + at) // segment
                tables = make_tables(
                    base_cos[0, g : g + 1, :], base_sin[0, g : g + 1, :], row_cos[...], row_sin[...]
                )
                part, into = slice(at, at + segment), slice(start + at, start + at + segment)
                kv_ref[0, dy, into, :128] = low(turn(kv[part, :128], tables, 1.0))
                kv_ref[0, dy, into, 128:256] = low(turn_mixed(kv[part, 128:256], tables, 1.0))
                if start + at == 0:
                    query = dot(normed[part], w_q)
                    query = jnp.concatenate(
                        [query, jnp.zeros((segment, 256 - width), f32)], axis=1
                    )
                    rows = slice(dy * segment, (dy + 1) * segment)
                    q_ref[0, rows, :128] = low(turn(query[:, :128], tables, 1.0) * SCALE)
                    last = low(turn(query[:, 128:], tables, 1.0) * SCALE)
                    q_ref[0, rows, 128:] = last[:, : width - 128]
            kv_ref[0, dy, here, 256:] = low(kv[:, 256:])


def project(index, a_all, b_all, bases, row_tables, gain, weights):
    slots, tokens, features = a_all.shape
    own = row_tables[0].shape[0]
    cols = weights[0].shape[1]
    width = cols // 3
    block = pl.BlockSpec((1, tokens, features), lambda i: (i, 0, 0))
    base = pl.BlockSpec((1,) + bases[0].shape[1:], lambda i: (i, 0, 0))
    wide = lambda n: pl.BlockSpec((1, 2, tokens, n), lambda i: (i, 0, 0, 0))
    return pl.pallas_call(
        project_kernel,
        grid=(slots,),
        in_specs=[IN_SMEM, block, block, base, base] + [IN_VMEM] * 7,
        out_specs=[
            wide(features),
            wide(2 * width),
            pl.BlockSpec((1, 2 * own, width), lambda i: (i, 0, 0)),
        ],
        out_shape=[
            jax.ShapeDtypeStruct((slots, 2, tokens, features), bf16),
            jax.ShapeDtypeStruct((slots, 2, tokens, 2 * width), bf16),
            jax.ShapeDtypeStruct((slots, 2 * own, width), bf16),
        ],
        scratch_shapes=[pltpu.VMEM((features, cols), bf16)],
        compiler_params=params(),
        name="project",
    )(index, a_all, b_all, *bases, *row_tables, gain, *weights)


def middle_kernel(
    index_ref, a_ref, b_ref, t0, t1, t2, t3, wa0, wa1, wa2, wa3, gain_ref,
    wi0, wi1, wi2, wi3, w_out_ref, c0, c1, c2, c3,
    send_ref, keep_ref, send_o_ref, keep_o_ref, mid_ref, normed_ref, hidden_ref, ggu_ref,
    gain_part_ref, w_scr, up_scr,
):
    attn, w_attn, cot = (t0, t1, t2, t3), (wa0, wa1, wa2, wa3), (c0, c1, c2, c3)
    own = a_ref.shape[1]
    tok = 2 * own
    ff = w_out_ref.shape[0]
    in_row_order(index_ref, (wi0, wi1, wi2, wi3), w_scr)
    up_scr[...] = w_scr[:, ff:]
    gain = gain_ref[...]
    gain_part = jnp.zeros(gain.shape, f32)
    for dc in (1, 0):
        rows = slice(dc * 2 * tok, (dc + 1) * 2 * tok)
        mid = jnp.concatenate(
            [r[2 * dc + dx] for dx in range(2) for r in (a_ref, b_ref)]
        ).astype(f32)
        for d in range(4):
            part = [
                attn[d][(d ^ (2 * dc + dx)) * tok : ((d ^ (2 * dc + dx)) + 1) * tok, :]
                for dx in range(2)
            ]
            mid = mid + dot(jnp.concatenate(part), w_attn[d][...])
        xhat, _ = norm_parts(mid)
        normed = low(xhat * gain)
        normed_ref[rows, :] = normed
        w_gate, w_up = w_scr[:, :ff], up_scr[...]
        gate, up = dot(normed, w_gate), dot(normed, w_up)
        cdf, pdf = phi_parts(gate)
        act = gate * cdf
        hidden = low(act * up)
        hidden_ref[rows, :] = hidden
        grad_out = jnp.concatenate([cot[2 * dc][...], cot[2 * dc + 1][...]])
        grad_hidden = dot_nt(grad_out, w_out_ref[...])
        grad_gate = low(grad_hidden * up * (cdf + gate * pdf))
        grad_up = low(grad_hidden * act)
        ggu_ref[rows, :ff] = grad_gate
        ggu_ref[rows, ff:] = grad_up
        part_normed = dot_nt(grad_gate, w_gate) + dot_nt(grad_up, w_up)
        gain_part = gain_part + jnp.sum(part_normed * xhat, axis=0, keepdims=True)
        out_part = dot(hidden, w_out_ref[...])
        if dc:
            send_ref[...] = low(part_normed)
            send_o_ref[...] = low(out_part)
        else:
            keep_ref[...] = part_normed
            keep_o_ref[:tok, :] = out_part[:tok] + mid[:tok]
            keep_o_ref[tok:, :] = out_part[tok:]
            mid_ref[...] = mid
    gain_part_ref[...] = gain_part


def middle_part(index, a_all, b_all, rows, attn, w_attn, gain, w_in, w_out, cot):
    features = gain.shape[1]
    group, ff = attn[0].shape[0], w_out.shape[0]
    half = group // 2
    own = pl.BlockSpec((4, rows, features), lambda i: (0, 0, 0))
    flat = lambda v: pl.BlockSpec(v.shape, lambda i: (0, 0))
    others = [*attn, *w_attn, gain, *w_in, w_out, *cot]
    shapes = [
        ((half, features), bf16), ((half, features), f32),
        ((half, features), bf16), ((half, features), f32),
        ((half, features), f32), ((group, features), bf16),
        ((group, ff), bf16), ((group, 2 * ff), bf16), ((1, features), f32),
    ]
    return pl.pallas_call(
        middle_kernel,
        grid=(1,),
        in_specs=[IN_SMEM, own, own] + [flat(v) for v in others],
        out_specs=[pl.BlockSpec(shape, lambda i: (0, 0)) for shape, _ in shapes],
        out_shape=[jax.ShapeDtypeStruct(*s) for s in shapes],
        scratch_shapes=[pltpu.VMEM((features, 2 * ff), bf16), pltpu.VMEM((features, ff), bf16)],
        compiler_params=params(),
        name="middle_part",
    )(index, a_all, b_all, *others)


def branch_kernel(half_ref, x_ref, mid_ref, c0, c1, gain_ref, branch_ref, grad_ref):
    tok = c0.shape[0]
    for dx, cot in enumerate((c0, c1)):
        rows = slice(dx * tok, (dx + 1) * tok)
        there = slice((1 - dx) * tok, (2 - dx) * tok)
        grad_normed = half_ref[rows, :] + x_ref[there, :].astype(f32)
        xhat, inv = norm_parts(mid_ref[rows, :])
        grad = cot[...].astype(f32) + norm_back(grad_normed, gain_ref[...], xhat, inv)
        branch_ref[rows, :] = low(grad)
        if dx == 0:
            grad_ref[...] = grad


def branch(half_sum, from_x, mid, cot, gain):
    tok, features = cot[0].shape
    return pl.pallas_call(
        branch_kernel,
        in_specs=[IN_VMEM] * 6,
        out_specs=[IN_VMEM] * 2,
        out_shape=[
            jax.ShapeDtypeStruct((2 * tok, features), bf16),
            jax.ShapeDtypeStruct((tok, features), f32),
        ],
        compiler_params=params(),
        name="branch",
    )(half_sum, from_x, mid, cot[0], cot[1], gain)


def tokens_back_kernel(
    index_ref, dkv_ref, dq_ref, a_ref, b_ref, w0, w1, w2, w3, part_ref, gain_ref, w_scr
):
    segment = part_ref.shape[3]
    tokens = a_ref.shape[1]
    width = dq_ref.shape[2]

    @pl.when(pl.program_id(0) == 0)
    def _():
        in_row_order(index_ref, (w0, w1, w2, w3), w_scr)
        gain_ref[...] = jnp.zeros(gain_ref.shape, f32)

    w_kv, w_q = w_scr[:, : 2 * width], w_scr[:, 2 * width :]
    block = min(256, tokens)
    total = jnp.zeros(gain_ref.shape, f32)
    for dy, ref in enumerate((a_ref, b_ref)):
        for start in range(0, tokens, block):
            here = slice(start, start + block)
            part = dot_nt(dkv_ref[0, dy, here, :], w_kv)
            if start == 0:
                own = dot_nt(dq_ref[0, dy * segment : (dy + 1) * segment, :], w_q)
                part = jnp.concatenate([part[:segment] + own, part[segment:]])
            xhat, _ = norm_parts(ref[0, here, :].astype(f32))
            total = total + jnp.sum(part * xhat, axis=0, keepdims=True)
            for at in range(0, block, segment):
                g = (start + at) // segment
                part_ref[0, g, dy, :, :] = part[at : at + segment].astype(part_ref.dtype)
    gain_ref[...] += total


def tokens_back(index, first, d_kv, d_query, a_all, b_all, weights, segment, dtype):
    slots, tokens, features = a_all.shape
    cols = weights[0].shape[1]
    block = pl.BlockSpec((1, tokens, features), lambda i: (i + first, 0, 0))
    count = tokens // segment
    out_block = (1, count, 2, segment, features)
    return pl.pallas_call(
        tokens_back_kernel,
        grid=(2,),
        in_specs=[
            IN_SMEM,
            pl.BlockSpec((1,) + d_kv.shape[1:], lambda i: (i + first, 0, 0, 0)),
            pl.BlockSpec((1,) + d_query.shape[1:], lambda i: (i + first, 0, 0)),
            block,
            block,
        ]
        + [IN_VMEM] * 4,
        out_specs=[
            pl.BlockSpec(out_block, lambda i: (i, 0, 0, 0, 0)),
            pl.BlockSpec((1, features), lambda i: (0, 0)),
        ],
        out_shape=[
            jax.ShapeDtypeStruct((2,) + out_block[1:], dtype),
            jax.ShapeDtypeStruct((1, features), f32),
        ],
        scratch_shapes=[pltpu.VMEM((features, cols), bf16)],
        compiler_params=params(),
        name="tokens_back",
    )(index, d_kv, d_query, a_all, b_all, *weights)


def local(tokens, gain_attn, gain_ffn, w_qkv, w_attn, w_in, w_out, cotangent):
    seq_count, rows, features = tokens.shape
    z_count = lax.axis_size("z")
    x_index, c_index = lax.axis_index("x"), lax.axis_index("core")
    z_index, y_index = lax.axis_index("z"), lax.axis_index("y")
    shard = 2 * x_index + c_index
    shards = 4
    tok = 2 * rows
    group = shards * tok
    width = (HEADS // shards) * HEAD_DIM
    ff = w_out.shape[0]
    w_rows = w_qkv.shape[0]
    slot_of = jnp.take(jnp.array(SLOT_SHARD), jnp.arange(shards) ^ shard)
    index = jnp.stack([shard, y_index]).astype(jnp.int32)

    both = jnp.stack([tokens, cotangent], axis=1)
    mine, theirs = pick(both, y_index), pick(both, 1 - y_index)
    got = swap(theirs, "y")

    def gather_all(piece):
        piece = piece[None]
        for bit in reversed(z_bits()):
            piece = jnp.concatenate([piece, swap_z(piece, bit)])
        piece = jnp.concatenate([piece, swap(piece, "x")])
        piece = jnp.concatenate([piece, swap(piece, "core")])
        return piece.reshape(shards, z_count * rows, features)

    qkv_parts, in_parts = prepare(index, w_qkv, w_in)
    a_all = gather_all(mine[0])
    qkv_parts = exchange_shard(qkv_parts)
    b_all = gather_all(got[0])
    cot = gather_shard(jnp.concatenate([mine[1], got[1]]))
    in_parts = exchange_shard(in_parts)
    attn_parts = gather_shard(w_attn)
    gain_a, gain_f = gain_attn.reshape(1, features), gain_ffn.reshape(1, features)

    z_of = (z_index ^ jnp.array(z_offsets()))[None, None, :]
    s_of = (shard ^ jnp.array(SLOT_SHARD))[:, None, None]
    y_of = (y_index ^ jnp.arange(2))[None, :, None]
    place = ((2 * z_of + y_of) * shards + s_of) * rows
    inverse_freq = jnp.exp(
        (jnp.arange(128) % HALF).astype(f32) * (-1.0 / HALF) * jnp.log(jnp.float32(rope_base))
    )
    base_angles = place[..., None].astype(f32) * inverse_freq
    row_angles = jnp.arange(rows, dtype=f32)[:, None] * inverse_freq
    bases = (jnp.cos(base_angles), jnp.sin(base_angles))
    row_tables = (jnp.cos(row_angles), jnp.sin(row_angles))
    q_bases = tuple(b[:, :, 0].reshape(-1, 128) for b in bases)
    slot_bases = tuple(b.reshape(shards, -1, 128) for b in bases)
    flat_bases = tuple(b.reshape(-1, 128) for b in bases)

    normed_a, kv, query = project(index, a_all, b_all, slot_bases, row_tables, gain_a, qkv_parts)
    query = query.reshape(group, width)
    attn, attn_low, lse = attend(query, kv.reshape(-1, 2 * width))

    got_attn = gather_shard(attn_low)
    send, keep, send_o, keep_o, mid, normed_f, hidden, grad_gate_up, gain_f_part = middle_part(
        index, a_all, b_all, rows, got_attn, attn_parts, gain_f, in_parts, w_out, cot
    )

    half_sum = keep + swap(send, "core").astype(f32)
    half_branch, grad_middle = branch(half_sum, swap(low(half_sum), "x"), mid, cot, gain_f)
    other = swap(half_branch, "core")
    d_kv, d_query = attend_back(
        query, kv.reshape(-1, 2 * width), half_branch, other, w_attn, attn, lse,
        flat_bases, q_bases, row_tables,
    )

    d_kv_slots = d_kv.reshape(kv.shape)
    d_query_slots = d_query.reshape(shards, tok, width)
    back = lambda first, dtype: tokens_back(
        index, first, d_kv_slots, d_query_slots, a_all, b_all, qkv_parts, rows, dtype
    )
    far, gain_far = back(2, bf16)
    near, gain_near = back(0, bf16)
    near = near.astype(f32) + swap(far, "core").astype(f32)
    near = near[0] + swap(low(near[1]), "x").astype(f32)
    for bit in z_bits():
        near = near.reshape((2, -1) + near.shape[1:])
        near = near[0] + swap_z(low(near[1]), bit).astype(f32)
    own = near.reshape(tok, features)
    gain_a_part = gain_far + gain_near

    grad_branch = jnp.concatenate([half_branch, other])
    d_in = dot_tn(normed_f, grad_gate_up)
    d_out = dot_tn(hidden, jnp.concatenate(cot))
    d_attn = dot_tn(attn_low, grad_branch)
    own_normed = normed_a[:, :, :rows].reshape(group, features)
    d_qkv = jnp.concatenate(
        [dot_tn(own_normed, d_query), dot_tn(normed_a.reshape(-1, features), d_kv)], axis=1
    )

    xhat_own, inv_own = norm_parts(jnp.concatenate([a_all[0, :rows], b_all[0, :rows]]).astype(f32))
    grad_tokens = grad_middle + norm_back(own, gain_attn, xhat_own, inv_own)
    out_near = keep_o + swap(send_o, "core").astype(f32)
    out_own = out_near[:tok] + swap(low(out_near[tok:]), "x").astype(f32)
    results = low(jnp.stack([out_own, grad_tokens])).reshape(2, 2, rows, features)
    from_y = swap(results[:, 1], "y")
    output = pair_in_order(results[0, 0], from_y[0], y_index)
    grad_tokens = pair_in_order(results[1, 0], from_y[1], y_index)

    def from_columns(grad, thirds):
        lead = w_rows // (2 * z_count)
        cut = grad.reshape(shards, 2 * z_count, lead, -1).transpose(1, 0, 2, 3)
        total = low(ctx_sum(cut, z_index, y_index))
        parts = exchange_shard([pick(total, shard ^ SLOT_SHARD[e]) for e in range(4)])
        parts = jnp.take(jnp.stack(parts), slot_of, axis=0)
        parts = parts.reshape(shards, lead, thirds, -1).transpose(1, 2, 0, 3).reshape(lead, -1)
        return ctx_gather(parts, z_index, y_index).reshape(w_rows, -1).astype(f32)

    rows_grad = jnp.concatenate([d_out, d_attn])
    rows_grad = jnp.pad(rows_grad, ((0, -rows_grad.shape[0] % (2 * z_count)), (0, 0)))
    rows_grad = rows_grad.reshape(2 * z_count, -1, features)
    rows_grad = ctx_gather(low(ctx_sum(rows_grad, z_index, y_index)), z_index, y_index)
    rows_grad = rows_grad.reshape(-1, features).astype(f32)

    gains = jnp.concatenate([gain_a_part, gain_f_part])
    for axis in ("core", "x", "y"):
        gains = gains + swap(gains, axis)
    for bit in z_bits():
        gains = gains + swap_z(gains, bit)

    return (
        output,
        grad_tokens,
        gains[0],
        gains[1],
        from_columns(d_qkv, 3),
        rows_grad[ff : ff + w_rows],
        from_columns(d_in, 2),
        rows_grad[:ff],
    )


def solution(mesh):
    shards, cycle = mesh.shape["shard"], mesh.shape["ctx"]
    fine = Mesh(mesh.devices.reshape(shards // 2, 2, cycle // 2, 2), ("x", "core", "z", "y"))
    by_token = P(None, ("z", "y", "x", "core"), None)
    by_row = P(("x", "core"), None)
    return jax.shard_map(
        local,
        mesh=fine,
        in_specs=(by_token, P(), P(), by_row, by_row, by_row, by_row, by_token),
        out_specs=(by_token, by_token, P(), P(), by_row, by_row, by_row, by_row),
        check_vma=False,
    )
```

```python
import functools

import jax
import jax.numpy as jnp
from jax import lax
from jax.experimental import pallas as pl
from jax.experimental.pallas import tpu as pltpu
from jax.sharding import Mesh, PartitionSpec as P

HEADS = 12
HEAD_DIM = 64
HALF = HEAD_DIM // 2
SCALE = HEAD_DIM ** (-0.5)

epsilon = 1e-05
rope_base = 160000.0
f32 = jnp.float32
bf16 = jnp.bfloat16
VMEM_LIMIT = 56 * 2**20


def low(v):
    return v.astype(bf16)


def swap(v, axis):
    return lax.ppermute(v, axis, [(0, 1), (1, 0)])


def swap_z(v, bit):
    count = lax.axis_size("z")
    return lax.ppermute(v, "z", [(i, i ^ bit) for i in range(count)])


def across(v):
    return lax.ppermute(v, ("x", "core"), [(i, 3 - i) for i in range(4)])


def z_bits():
    bits, bit = [], 1
    while bit < lax.axis_size("z"):
        bits.append(bit)
        bit *= 2
    return bits


def z_offsets():
    offsets = [0]
    for bit in reversed(z_bits()):
        offsets = offsets + [o ^ bit for o in offsets]
    return offsets


SLOT_SHARD = [2 * (e & 1) + (e >> 1) for e in range(4)]


def gather_shard(v):
    from_x = swap(v, "x")
    from_core = swap(v, "core")
    return [v, from_x, from_core, swap(from_x, "core")]


def exchange_shard(parts):
    return [parts[0], swap(parts[1], "x"), swap(parts[2], "core"), across(parts[3])]


def after(value, *others):
    return lax.optimization_barrier((value, others))[0]


def pick(v, index):
    return lax.dynamic_index_in_dim(v, index, 0, keepdims=False)


def pair_in_order(own, other, bit):
    return jnp.where(bit == 0, jnp.stack([own, other]), jnp.stack([other, own]))


def first_half(value, bit):
    value = value.reshape((2, -1) + value.shape[1:])
    return pick(value, bit), low(pick(value, 1 - bit))


def next_half(kept, got, bit):
    kept = kept.reshape((2, -1) + kept.shape[1:])
    got = got.reshape(kept.shape)
    total = lambda at: pick(kept, at) + pick(got, at).astype(f32)
    return total(bit), low(total(1 - bit))


def reversed_bits(z):
    bits = z_bits()
    return sum(((z // bit) % 2) * back for bit, back in zip(bits, reversed(bits)))


def norm_parts(values):
    centre = jnp.mean(values, axis=-1, keepdims=True)
    shifted = values - centre
    spread = jnp.mean(shifted * shifted, axis=-1, keepdims=True)
    inv = lax.rsqrt(spread + epsilon)
    return shifted * inv, inv


def norm_back(grad_normed, gain, xhat, inv):
    e = grad_normed * gain
    return inv * (
        e
        - jnp.mean(e, axis=-1, keepdims=True)
        - xhat * jnp.mean(e * xhat, axis=-1, keepdims=True)
    )


def dot(a, b):
    return jnp.dot(a, b, preferred_element_type=f32)


def dot_nt(a, b):
    return lax.dot_general(a, b, (((1,), (1,)), ((), ())), preferred_element_type=f32)


def dot_tn(a, b):
    return lax.dot_general(a, b, (((0,), (0,)), ((), ())), preferred_element_type=f32)


def phi_parts(gate):
    cdf = 0.5 * (1.0 + lax.erf(gate * (0.5**0.5)))
    pdf = jnp.exp(-0.5 * gate * gate) * 0.3989422804014327
    return cdf, pdf


def turn(u, tables, sign):
    cosine, sine_low, sine_high = tables
    turned = pltpu.roll(u, 96, 1) * sine_low + pltpu.roll(u, 32, 1) * sine_high
    return u * cosine + sign * turned


def make_tables(base_cos, base_sin, row_cos, row_sin):
    cosine = base_cos * row_cos - base_sin * row_sin
    sine = base_sin * row_cos + base_cos * row_sin
    is_low = lax.broadcasted_iota(jnp.int32, sine.shape, 1) % HEAD_DIM < HALF
    return cosine, jnp.where(is_low, -sine, 0.0), jnp.where(is_low, 0.0, sine)


def turn_mixed(u, tables, sign):
    is_key = lax.broadcasted_iota(jnp.int32, u.shape, 1) < HEAD_DIM
    return jnp.where(is_key, turn(u, tables, sign), u)


def in_row_order(index_ref, parts, scratch):
    rows = parts[0].shape[0]
    for e, part in enumerate(parts):
        at = pl.multiple_of((index_ref[0] ^ SLOT_SHARD[e]) * rows, rows)
        scratch[pl.ds(at, rows), :] = part[...]


def cost(microseconds):
    return pl.CostEstimate(
        flops=int(microseconds * 1e9), transcendentals=0, bytes_accessed=int(microseconds * 3e6)
    )


def params():
    return pltpu.CompilerParams(vmem_limit_bytes=VMEM_LIMIT)


IN_SMEM = pl.BlockSpec(memory_space=pltpu.SMEM)
IN_VMEM = pl.BlockSpec(memory_space=pltpu.VMEM)


def prepare_kernel(order, index_ref, w_ref, *outs):
    part = w_ref.shape[1] // (4 * len(order))
    for s in range(4):

        @pl.when(index_ref[0] == s)
        def _():
            for e in range(4):
                t = s ^ SLOT_SHARD[e]
                for place, third in enumerate(order):
                    at = (third * 4 + t) * part
                    outs[e][:, place * part : (place + 1) * part] = w_ref[:, at : at + part]


def prepare(index, weight, order):
    shape = jax.ShapeDtypeStruct((weight.shape[0], weight.shape[1] // 4), bf16)
    return pl.pallas_call(
        functools.partial(prepare_kernel, order),
        out_shape=[shape] * 4,
        in_specs=[IN_SMEM, IN_VMEM],
        out_specs=[IN_VMEM] * 4,
        compiler_params=params(),
        name="prepare",
        cost_estimate=cost(2.4),
    )(index, weight)


def attend_kernel(q_ref, kv_ref, attn_ref, low_ref, lse_ref, max_ref, sum_ref, acc_ref):
    at = pl.program_id(0)
    heads = q_ref.shape[1] // HEAD_DIM
    width = heads * HEAD_DIM

    @pl.when(at == 0)
    def _():
        max_ref[...] = jnp.full(max_ref.shape, -1e30, f32)
        sum_ref[...] = jnp.zeros(sum_ref.shape, f32)
        acc_ref[...] = jnp.zeros(acc_ref.shape, f32)

    block = min(256, q_ref.shape[0])
    for h in range(heads):
        cols = slice(h * HEAD_DIM, (h + 1) * HEAD_DIM)
        key = kv_ref[:, cols]
        value = kv_ref[:, width + h * HEAD_DIM : width + (h + 1) * HEAD_DIM]
        for start in range(0, q_ref.shape[0], block):
            rows = slice(start, start + block)
            scores = dot_nt(q_ref[rows, cols], key)
            old = max_ref[rows, h : h + 1]
            new = jnp.maximum(old, jnp.max(scores, axis=1, keepdims=True))
            weights = jnp.exp(scores - new)
            factor = jnp.exp(old - new)
            max_ref[rows, h : h + 1] = new
            total = sum_ref[rows, h : h + 1] * factor + jnp.sum(weights, axis=1, keepdims=True)
            sum_ref[rows, h : h + 1] = total
            acc = acc_ref[rows, cols] * factor + dot(low(weights), value)
            acc_ref[rows, cols] = acc

    @pl.when(at == pl.num_programs(0) - 1)
    def _():
        for h in range(heads):
            cols = slice(h * HEAD_DIM, (h + 1) * HEAD_DIM)
            attn = acc_ref[:, cols] / sum_ref[:, h : h + 1]
            attn_ref[:, cols] = attn
            low_ref[:, cols] = low(attn)
            lse_ref[:, h : h + 1] = max_ref[:, h : h + 1] + jnp.log(sum_ref[:, h : h + 1])


def attend(query, kv):
    rows, width = query.shape
    chunk = min(2048, kv.shape[0])
    fixed = lambda shape: pl.BlockSpec(shape, lambda i: (0, 0))
    return pl.pallas_call(
        attend_kernel,
        grid=(kv.shape[0] // chunk,),
        in_specs=[fixed((rows, width)), pl.BlockSpec((chunk, 2 * width), lambda i: (i, 0))],
        out_specs=[fixed((rows, width)), fixed((rows, width)), fixed((rows, 128))],
        out_shape=[
            jax.ShapeDtypeStruct((rows, width), f32),
            jax.ShapeDtypeStruct((rows, width), bf16),
            jax.ShapeDtypeStruct((rows, 128), f32),
        ],
        scratch_shapes=[
            pltpu.VMEM((rows, 128), f32),
            pltpu.VMEM((rows, 128), f32),
            pltpu.VMEM((rows, width), f32),
        ],
        compiler_params=pltpu.CompilerParams(vmem_limit_bytes=VMEM_LIMIT),
        name="attend",
        cost_estimate=cost(8.4),
    )(query, kv)


def attend_back_kernel(
    q_ref, kv_ref, half_ref, other_ref, w_ref, attn_ref, lse_ref,
    base_cos, base_sin, q_base_cos, q_base_sin, row_cos, row_sin,
    dkv_ref, dq_ref, dq_scr, dkv_scr, lse_scr, delta_scr, grad_scr,
):
    at = pl.program_id(0)
    width = q_ref.shape[1]
    heads = width // HEAD_DIM
    keys = kv_ref.shape[0]
    block = min(512, keys)
    segment = row_cos.shape[0]

    @pl.when(at == 0)
    def _():
        half = half_ref.shape[0]
        grad_scr[:half, :] = low(dot_nt(half_ref[...], w_ref[...]))
        grad_scr[half:, :] = low(dot_nt(other_ref[...], w_ref[...]))
        dq_scr[...] = jnp.zeros(dq_scr.shape, f32)
        lse_scr[...] = lse_ref[...].T
        for h in range(heads):
            cols = slice(h * HEAD_DIM, (h + 1) * HEAD_DIM)
            both = (grad_scr[:, cols].astype(f32) * attn_ref[:, cols]).T
            delta_scr[h : h + 1, :] = jnp.sum(both, axis=0, keepdims=True)

    for h in range(heads):
        cols = slice(h * HEAD_DIM, (h + 1) * HEAD_DIM)
        vcols = slice(width + h * HEAD_DIM, width + (h + 1) * HEAD_DIM)
        query, grad = q_ref[:, cols], grad_scr[:, cols]
        lse, delta = lse_scr[h : h + 1, :], delta_scr[h : h + 1, :]

        def step(i, carry):
            rows = pl.ds(i * block, block)
            key, value = kv_ref[rows, cols], kv_ref[rows, vcols]
            probs = jnp.exp(dot_nt(key, query) - lse)
            dkv_scr[rows, vcols] = dot(low(probs), grad)
            grad_scores = low(probs * (dot_nt(value, grad) - delta))
            dkv_scr[rows, cols] = dot(grad_scores, query)
            dq_scr[cols, :] += dot_tn(key, grad_scores)
            return carry

        lax.fori_loop(0, keys // block, step, 0)

    def finish(i, carry):
        rows = pl.ds(i * segment, segment)
        one = pl.ds(i, 1)
        tables = make_tables(base_cos[one, :], base_sin[one, :], row_cos[...], row_sin[...])
        dkv_ref[rows, :128] = low(turn(dkv_scr[rows, :128], tables, -1.0))
        dkv_ref[rows, 128:256] = low(turn_mixed(dkv_scr[rows, 128:256], tables, -1.0))
        dkv_ref[rows, 256:] = low(dkv_scr[rows, 256:])
        return carry

    lax.fori_loop(0, keys // segment, finish, 0)

    @pl.when(at == pl.num_programs(0) - 1)
    def _():
        first = dq_scr[:128, :].T * SCALE
        second = dq_scr[128:, :].T * SCALE
        for g in range(q_base_cos.shape[0]):
            rows = slice(g * segment, (g + 1) * segment)
            tables = make_tables(
                q_base_cos[g : g + 1, :], q_base_sin[g : g + 1, :], row_cos[...], row_sin[...]
            )
            dq_ref[rows, :128] = low(turn(first[rows], tables, -1.0))
            dq_ref[rows, 128:] = low(turn(second[rows], tables, -1.0)[:, : width - 128])


def attend_back(query, kv, half, other, w_attn, attn, lse, bases, q_bases, row_tables):
    rows, width = query.shape
    chunk = min(2048, kv.shape[0])
    segments = chunk // row_tables[0].shape[0]
    fixed = lambda v: pl.BlockSpec(v.shape, lambda i: (0, 0))
    moving = lambda n, cols: pl.BlockSpec((n, cols), lambda i: (i, 0))
    still = (half, other, w_attn, attn, lse)
    return pl.pallas_call(
        attend_back_kernel,
        grid=(kv.shape[0] // chunk,),
        in_specs=[fixed(query), moving(chunk, 2 * width)]
        + [fixed(v) for v in still]
        + [moving(segments, 128)] * 2
        + [fixed(v) for v in q_bases + row_tables],
        out_specs=[moving(chunk, 2 * width), pl.BlockSpec((rows, width), lambda i: (0, 0))],
        out_shape=[
            jax.ShapeDtypeStruct(kv.shape, bf16),
            jax.ShapeDtypeStruct((rows, width), bf16),
        ],
        scratch_shapes=[
            pltpu.VMEM((256, rows), f32),
            pltpu.VMEM((chunk, 2 * width), f32),
            pltpu.VMEM((128, rows), f32),
            pltpu.VMEM((8, rows), f32),
            pltpu.VMEM((rows, width), bf16),
        ],
        compiler_params=params(),
        name="attend_back",
        cost_estimate=cost(18),
    )(query, kv, *still, *bases, *q_bases, *row_tables)


def project_kernel(
    index_ref, a_ref, b_ref, base_cos, base_sin, row_cos, row_sin, gain_ref, w0, w1, w2, w3,
    normed_ref, kv_ref, q_ref, w_scr,
):
    width = q_ref.shape[2]
    segment = row_cos.shape[0]

    @pl.when(pl.program_id(0) == 0)
    def _():
        in_row_order(index_ref, (w0, w1, w2, w3), w_scr)

    tokens = a_ref.shape[1]
    block = min(256, tokens)
    w_kv, w_q = w_scr[:, : 2 * width], w_scr[:, 2 * width :]
    for dy, ref in enumerate((a_ref, b_ref)):
        for start in range(0, tokens, block):
            here = slice(start, start + block)
            xhat, _ = norm_parts(ref[0, here, :].astype(f32))
            normed = low(xhat * gain_ref[...])
            normed_ref[0, dy, here, :] = normed
            kv = dot(normed, w_kv)
            for at in range(0, block, segment):
                g = dy * (tokens // segment) + (start + at) // segment
                tables = make_tables(
                    base_cos[0, g : g + 1, :], base_sin[0, g : g + 1, :], row_cos[...], row_sin[...]
                )
                part, into = slice(at, at + segment), slice(start + at, start + at + segment)
                kv_ref[0, dy, into, :128] = low(turn(kv[part, :128], tables, 1.0))
                kv_ref[0, dy, into, 128:256] = low(turn_mixed(kv[part, 128:256], tables, 1.0))
                if start + at == 0:
                    query = dot(normed[part], w_q)
                    query = jnp.concatenate(
                        [query, jnp.zeros((segment, 256 - width), f32)], axis=1
                    )
                    rows = slice(dy * segment, (dy + 1) * segment)
                    q_ref[0, rows, :128] = low(turn(query[:, :128], tables, 1.0) * SCALE)
                    last = low(turn(query[:, 128:], tables, 1.0) * SCALE)
                    q_ref[0, rows, 128:] = last[:, : width - 128]
            kv_ref[0, dy, here, 256:] = low(kv[:, 256:])


def project(index, a_all, b_all, bases, row_tables, gain, weights):
    slots, tokens, features = a_all.shape
    own = row_tables[0].shape[0]
    cols = weights[0].shape[1]
    width = cols // 3
    block = pl.BlockSpec((1, tokens, features), lambda i: (i, 0, 0))
    base = pl.BlockSpec((1,) + bases[0].shape[1:], lambda i: (i, 0, 0))
    wide = lambda n: pl.BlockSpec((1, 2, tokens, n), lambda i: (i, 0, 0, 0))
    return pl.pallas_call(
        project_kernel,
        grid=(slots,),
        in_specs=[IN_SMEM, block, block, base, base] + [IN_VMEM] * 7,
        out_specs=[
            wide(features),
            wide(2 * width),
            pl.BlockSpec((1, 2 * own, width), lambda i: (i, 0, 0)),
        ],
        out_shape=[
            jax.ShapeDtypeStruct((slots, 2, tokens, features), bf16),
            jax.ShapeDtypeStruct((slots, 2, tokens, 2 * width), bf16),
            jax.ShapeDtypeStruct((slots, 2 * own, width), bf16),
        ],
        scratch_shapes=[pltpu.VMEM((features, cols), bf16)],
        compiler_params=params(),
        name="project",
        cost_estimate=cost(7.5),
    )(index, a_all, b_all, *bases, *row_tables, gain, *weights)


def middle_kernel(
    index_ref, a_ref, b_ref, t0, t1, t2, t3, wa0, wa1, wa2, wa3, gain_ref,
    wi0, wi1, wi2, wi3, w_out_ref, c0, c1, c2, c3,
    send_ref, keep_ref, send_o_ref, keep_o_ref, mid_ref, normed_ref, hidden_ref, ggu_ref,
    gain_part_ref, w_scr, up_scr,
):
    attn, w_attn, cot = (t0, t1, t2, t3), (wa0, wa1, wa2, wa3), (c0, c1, c2, c3)
    own = a_ref.shape[1]
    tok = 2 * own
    ff = w_out_ref.shape[0]
    in_row_order(index_ref, (wi0, wi1, wi2, wi3), w_scr)
    up_scr[...] = w_scr[:, ff:]
    gain = gain_ref[...]
    gain_part = jnp.zeros(gain.shape, f32)
    for dc in (1, 0):
        rows = slice(dc * 2 * tok, (dc + 1) * 2 * tok)
        mid = jnp.concatenate(
            [r[2 * dc + dx] for dx in range(2) for r in (a_ref, b_ref)]
        ).astype(f32)
        for d in range(4):
            part = [
                attn[d][(d ^ (2 * dc + dx)) * tok : ((d ^ (2 * dc + dx)) + 1) * tok, :]
                for dx in range(2)
            ]
            mid = mid + dot(jnp.concatenate(part), w_attn[d][...])
        xhat, _ = norm_parts(mid)
        normed = low(xhat * gain)
        normed_ref[rows, :] = normed
        w_gate, w_up = w_scr[:, :ff], up_scr[...]
        gate, up = dot(normed, w_gate), dot(normed, w_up)
        cdf, pdf = phi_parts(gate)
        act = gate * cdf
        hidden = low(act * up)
        hidden_ref[rows, :] = hidden
        grad_out = jnp.concatenate([cot[2 * dc][...], cot[2 * dc + 1][...]])
        grad_hidden = dot_nt(grad_out, w_out_ref[...])
        grad_gate = low(grad_hidden * up * (cdf + gate * pdf))
        grad_up = low(grad_hidden * act)
        ggu_ref[rows, :ff] = grad_gate
        ggu_ref[rows, ff:] = grad_up
        part_normed = dot_nt(grad_gate, w_gate) + dot_nt(grad_up, w_up)
        gain_part = gain_part + jnp.sum(part_normed * xhat, axis=0, keepdims=True)
        out_part = dot(hidden, w_out_ref[...])
        if dc:
            send_ref[...] = low(part_normed)
            send_o_ref[...] = low(out_part)
        else:
            keep_ref[...] = part_normed
            keep_o_ref[:tok, :] = out_part[:tok] + mid[:tok]
            keep_o_ref[tok:, :] = out_part[tok:]
            mid_ref[...] = mid
    gain_part_ref[...] = gain_part


def middle_part(index, a_all, b_all, rows, attn, w_attn, gain, w_in, w_out, cot):
    features = gain.shape[1]
    group, ff = attn[0].shape[0], w_out.shape[0]
    half = group // 2
    own = pl.BlockSpec((4, rows, features), lambda i: (0, 0, 0))
    flat = lambda v: pl.BlockSpec(v.shape, lambda i: (0, 0))
    others = [*attn, *w_attn, gain, *w_in, w_out, *cot]
    shapes = [
        ((half, features), bf16), ((half, features), f32),
        ((half, features), bf16), ((half, features), f32),
        ((half, features), f32), ((group, features), bf16),
        ((group, ff), bf16), ((group, 2 * ff), bf16), ((1, features), f32),
    ]
    return pl.pallas_call(
        middle_kernel,
        grid=(1,),
        in_specs=[IN_SMEM, own, own] + [flat(v) for v in others],
        out_specs=[pl.BlockSpec(shape, lambda i: (0, 0)) for shape, _ in shapes],
        out_shape=[jax.ShapeDtypeStruct(*s) for s in shapes],
        scratch_shapes=[pltpu.VMEM((features, 2 * ff), bf16), pltpu.VMEM((features, ff), bf16)],
        compiler_params=params(),
        name="middle_part",
        cost_estimate=cost(8.6),
    )(index, a_all, b_all, *others)


def branch_kernel(half_ref, x_ref, mid_ref, c0, c1, gain_ref, branch_ref, grad_ref):
    tok = c0.shape[0]
    for dx, cot in enumerate((c0, c1)):
        rows = slice(dx * tok, (dx + 1) * tok)
        there = slice((1 - dx) * tok, (2 - dx) * tok)
        grad_normed = half_ref[rows, :] + x_ref[there, :].astype(f32)
        xhat, inv = norm_parts(mid_ref[rows, :])
        grad = cot[...].astype(f32) + norm_back(grad_normed, gain_ref[...], xhat, inv)
        branch_ref[rows, :] = low(grad)
        if dx == 0:
            grad_ref[...] = grad


def branch(half_sum, from_x, mid, cot, gain):
    tok, features = cot[0].shape
    return pl.pallas_call(
        branch_kernel,
        in_specs=[IN_VMEM] * 6,
        out_specs=[IN_VMEM] * 2,
        out_shape=[
            jax.ShapeDtypeStruct((2 * tok, features), bf16),
            jax.ShapeDtypeStruct((tok, features), f32),
        ],
        compiler_params=params(),
        name="branch",
        cost_estimate=cost(3),
    )(half_sum, from_x, mid, cot[0], cot[1], gain)


def tokens_back_kernel(
    index_ref, dkv_ref, dq_ref, a_ref, b_ref, w0, w1, w2, w3, part_ref, gain_ref, w_scr
):
    segment = part_ref.shape[3]
    tokens = a_ref.shape[1]
    width = dq_ref.shape[2]

    @pl.when(pl.program_id(0) == 0)
    def _():
        in_row_order(index_ref, (w0, w1, w2, w3), w_scr)
        gain_ref[...] = jnp.zeros(gain_ref.shape, f32)

    w_kv, w_q = w_scr[:, : 2 * width], w_scr[:, 2 * width :]
    block = min(256, tokens)
    total = jnp.zeros(gain_ref.shape, f32)
    for dy, ref in enumerate((a_ref, b_ref)):
        for start in range(0, tokens, block):
            here = slice(start, start + block)
            part = dot_nt(dkv_ref[0, dy, here, :], w_kv)
            if start == 0:
                own = dot_nt(dq_ref[0, dy * segment : (dy + 1) * segment, :], w_q)
                part = jnp.concatenate([part[:segment] + own, part[segment:]])
            xhat, _ = norm_parts(ref[0, here, :].astype(f32))
            total = total + jnp.sum(part * xhat, axis=0, keepdims=True)
            for at in range(0, block, segment):
                g = (start + at) // segment
                part_ref[0, g, dy, :, :] = part[at : at + segment].astype(part_ref.dtype)
    gain_ref[...] += total


def tokens_back(index, first, d_kv, d_query, a_all, b_all, weights, segment, dtype):
    slots, tokens, features = a_all.shape
    cols = weights[0].shape[1]
    block = pl.BlockSpec((1, tokens, features), lambda i: (i + first, 0, 0))
    count = tokens // segment
    out_block = (1, count, 2, segment, features)
    return pl.pallas_call(
        tokens_back_kernel,
        grid=(2,),
        in_specs=[
            IN_SMEM,
            pl.BlockSpec((1,) + d_kv.shape[1:], lambda i: (i + first, 0, 0, 0)),
            pl.BlockSpec((1,) + d_query.shape[1:], lambda i: (i + first, 0, 0)),
            block,
            block,
        ]
        + [IN_VMEM] * 4,
        out_specs=[
            pl.BlockSpec(out_block, lambda i: (i, 0, 0, 0, 0)),
            pl.BlockSpec((1, features), lambda i: (0, 0)),
        ],
        out_shape=[
            jax.ShapeDtypeStruct((2,) + out_block[1:], dtype),
            jax.ShapeDtypeStruct((1, features), f32),
        ],
        scratch_shapes=[pltpu.VMEM((features, cols), bf16)],
        compiler_params=params(),
        name="tokens_back",
        cost_estimate=cost(4.5),
    )(index, d_kv, d_query, a_all, b_all, *weights)


def chunk_row(index_ref, dy, offset, count, lead):
    chunk = (index_ref[1] ^ dy) * count + (index_ref[2] ^ offset)
    return pl.multiple_of(chunk * lead, lead)


def place_columns_kernel(parts, offsets, index_ref, own_ref, got_ref, out_ref):
    count, slots, lead, cols = own_ref.shape
    part = cols // parts
    for s in range(4):

        @pl.when(index_ref[0] == s)
        def _():
            for dy, ref in enumerate((own_ref, got_ref)):
                for j in range(count):
                    rows = pl.ds(chunk_row(index_ref, dy, offsets[j], count, lead), lead)
                    for e in range(slots):
                        t = s ^ SLOT_SHARD[e]
                        block = ref[j, e].astype(f32)
                        for p in range(parts):
                            at = (p * 4 + t) * part
                            out_ref[rows, at : at + part] = block[:, p * part : (p + 1) * part]


def place_rows_kernel(offsets, index_ref, own_ref, got_ref, first_ref, second_ref):
    count = own_ref.shape[0]
    lead = second_ref.shape[0] // (2 * count)
    first = own_ref.shape[1] - lead
    total = first_ref.shape[0]
    for dy, ref in enumerate((own_ref, got_ref)):
        for j in range(count):
            block = ref[j].astype(f32)
            at = chunk_row(index_ref, dy, offsets[j], count, first)
            second_ref[pl.ds(chunk_row(index_ref, dy, offsets[j], count, lead), lead), :] = block[
                first:
            ]

            @pl.when(at + first <= total)
            def _():
                first_ref[pl.ds(at, first), :] = block[:first]

            if total % first:

                @pl.when(at == total - total % first)
                def _():
                    first_ref[total - total % first :, :] = block[: total % first]


def place(kernel, index, own, got, shapes):
    return pl.pallas_call(
        kernel,
        in_specs=[IN_SMEM, IN_VMEM, IN_VMEM],
        out_specs=[IN_VMEM] * len(shapes),
        out_shape=[jax.ShapeDtypeStruct(shape, f32) for shape in shapes],
        compiler_params=params(),
        name="place",
        cost_estimate=cost(2.6),
    )(index, own, got)


def finish_kernel(near_ref, got_ref, a_ref, b_ref, grad_ref, gain_ref, out_ref):
    own = a_ref.shape[1]
    for dy, ref in enumerate((a_ref, b_ref)):
        rows = slice(dy * own, (dy + 1) * own)
        grad_normed = near_ref[rows, :] + got_ref[rows, :].astype(f32)
        xhat, inv = norm_parts(ref[0].astype(f32))
        grad = grad_ref[rows, :] + norm_back(grad_normed, gain_ref[...], xhat, inv)
        out_ref[rows, :] = low(grad)


def finish(near, got, a_all, b_all, grad_middle, gain, rows):
    features = gain.shape[1]
    own = pl.BlockSpec((1, rows, features), lambda i: (0, 0, 0))
    return pl.pallas_call(
        finish_kernel,
        grid=(1,),
        in_specs=[IN_VMEM, IN_VMEM, own, own, IN_VMEM, IN_VMEM],
        out_specs=IN_VMEM,
        out_shape=jax.ShapeDtypeStruct((2 * rows, features), bf16),
        compiler_params=params(),
        name="finish",
        cost_estimate=cost(2.4),
    )(near, got, a_all, b_all, grad_middle, gain)


def local(tokens, gain_attn, gain_ffn, w_qkv, w_attn, w_in, w_out, cotangent):
    seq_count, rows, features = tokens.shape
    z_count = lax.axis_size("z")
    x_index, c_index = lax.axis_index("x"), lax.axis_index("core")
    z_index, y_index = lax.axis_index("z"), lax.axis_index("y")
    shard = 2 * x_index + c_index
    shards = 4
    tok = 2 * rows
    group = shards * tok
    width = (HEADS // shards) * HEAD_DIM
    ff = w_out.shape[0]
    w_rows = w_qkv.shape[0]
    slot_of = jnp.take(jnp.array(SLOT_SHARD), jnp.arange(shards) ^ shard)
    index = jnp.stack([shard, y_index, reversed_bits(z_index)]).astype(jnp.int32)

    a_piece = pick(tokens, y_index)
    b_piece = swap(pick(tokens, 1 - y_index), "y")

    def gather_z(piece):
        piece = piece[None]
        for bit in reversed(z_bits()):
            piece = jnp.concatenate([piece, swap_z(piece, bit)])
        return piece

    def gather_core(piece, from_x):
        piece = jnp.concatenate([piece, from_x])
        piece = jnp.concatenate([piece, swap(piece, "core")])
        return piece.reshape(shards, z_count * rows, features)

    qkv_parts = exchange_shard(prepare(index, w_qkv, (1, 2, 0)))
    a_column = gather_z(a_piece)
    a_from_x = swap(a_column, "x")
    b_column = gather_z(b_piece)
    b_from_x = swap(after(b_column, qkv_parts[1:]), "x")
    a_all, b_all = gather_core(a_column, a_from_x), gather_core(b_column, b_from_x)

    w_in_late, w_attn_late, cot_late = after((w_in, w_attn, cotangent), b_from_x)
    cot_own = pick(cot_late, y_index)
    cot_own = jnp.concatenate([cot_own, swap(pick(cot_late, 1 - y_index), "y")])
    in_parts = exchange_shard(prepare(index, w_in_late, (0, 1)))
    late = (w_attn_late, cot_own)
    late_x, late_core = [swap(v, "x") for v in late], [swap(v, "core") for v in late]
    gain_a, gain_f = gain_attn.reshape(1, features), gain_ffn.reshape(1, features)

    z_of = (z_index ^ jnp.array(z_offsets()))[None, None, :]
    s_of = (shard ^ jnp.array(SLOT_SHARD))[:, None, None]
    y_of = (y_index ^ jnp.arange(2))[None, :, None]
    starts = ((2 * z_of + y_of) * shards + s_of) * rows
    inverse_freq = jnp.exp(
        (jnp.arange(128) % HALF).astype(f32) * (-1.0 / HALF) * jnp.log(jnp.float32(rope_base))
    )
    base_angles = starts[..., None].astype(f32) * inverse_freq
    row_angles = jnp.arange(rows, dtype=f32)[:, None] * inverse_freq
    bases = (jnp.cos(base_angles), jnp.sin(base_angles))
    row_tables = (jnp.cos(row_angles), jnp.sin(row_angles))
    q_bases = tuple(b[:, :, 0].reshape(-1, 128) for b in bases)
    slot_bases = tuple(b.reshape(shards, -1, 128) for b in bases)
    flat_bases = tuple(b.reshape(-1, 128) for b in bases)

    normed_a, kv, query = project(index, a_all, b_all, slot_bases, row_tables, gain_a, qkv_parts)
    query = query.reshape(group, width)
    attn, attn_low, lse = attend(after(query, in_parts[1:]), kv.reshape(-1, 2 * width))
    attn_low = after(attn_low, late_x, late_core)
    attn_parts, cot = (
        [own, x, core, swap(after(x, lse), "core")]
        for own, x, core in zip(late, late_x, late_core)
    )

    got_attn = gather_shard(attn_low)
    send, keep, send_o, keep_o, mid, normed_f, hidden, grad_gate_up, gain_f_part = middle_part(
        index, a_all, b_all, rows, got_attn, attn_parts, gain_f, in_parts, w_out, cot
    )

    half_sum = keep + swap(send, "core").astype(f32)
    half_low = low(half_sum)
    from_x = swap(half_low, "x")

    def by_block(grad):
        lead = w_rows // (2 * z_count)
        return grad.reshape(shards, 2 * z_count, lead, -1).transpose(1, 0, 2, 3)

    normed_f, grad_gate_up, hidden = after((normed_f, grad_gate_up, hidden), half_low)
    in_kept, in_sent = first_half(by_block(dot_tn(normed_f, grad_gate_up)), y_index)
    in_got = swap(in_sent, "y")
    d_out = dot_tn(hidden, jnp.concatenate(cot))
    out_lead = 8 * pl.cdiv(ff, 16 * z_count)

    mid = after(mid, in_sent)
    half_branch, grad_middle = branch(half_sum, from_x, mid, cot, gain_f)
    other = swap(half_branch, "core")

    bits = z_bits()
    z_bit = lambda bit: (z_index // bit) % 2
    in_got = after(in_got, half_branch)
    in_kept, in_sent = next_half(in_kept, in_got, z_bit(bits[0]))
    in_got = swap_z(in_sent, bits[0])
    d_attn = dot_tn(attn_low, jnp.concatenate([half_branch, other]))
    rows_grad = jnp.concatenate(
        [
            jnp.pad(d_out, ((0, 2 * z_count * out_lead - ff), (0, 0))).reshape(
                2 * z_count, out_lead, features
            ),
            d_attn.reshape(2 * z_count, -1, features),
        ],
        axis=1,
    )
    rows_kept, rows_sent = first_half(rows_grad, y_index)
    rows_got = swap(rows_sent, "y")
    out_got = swap(send_o, "core")
    kv_late = after(kv, rows_sent, in_sent)

    d_kv, d_query = attend_back(
        query, kv_late.reshape(-1, 2 * width), half_branch, other, w_attn, attn, lse,
        flat_bases, q_bases, row_tables,
    )
    turn_of = [d_query]

    def step(function, *values):
        values = after(values, turn_of[0])
        result = function(*values)
        turn_of[0] = result[-1] if isinstance(result, tuple) else result
        return result

    def z_step(kept, got, bit):
        kept, sent = step(lambda k, g: next_half(k, g, z_bit(bit)), kept, got)
        return kept, swap_z(sent, bit)

    def total(kept, got):
        return step(lambda k, g: low(k[0] + g[0].astype(f32)), kept, got)

    def to_owners(value):
        parts = [pick(value, shard ^ SLOT_SHARD[e]) for e in range(4)]
        return jnp.stack(exchange_shard(parts))

    def z_spread(value, bit):
        return step(lambda v, g: jnp.concatenate([v, g]), value, swap_z(value, bit))

    def token_step(kept, got, exchange):
        def add(k, g):
            k = k.reshape((2, -1) + k.shape[1:])
            g = g.reshape(k.shape)
            return k[0] + g[0].astype(f32), low(k[1] + g[1].astype(f32))

        kept, sent = step(add, kept, got)
        return kept, exchange(sent)

    d_kv_slots = d_kv.reshape(kv.shape)
    d_query_slots = d_query.reshape(shards, tok, width)
    back = lambda first, d, dtype: tokens_back(
        index, first, d, d_query_slots, a_all, b_all, qkv_parts, rows, dtype
    )
    d_kv_slots = after(d_kv_slots, out_got)
    far, gain_far = back(2, d_kv_slots, bf16)
    turn_of[0] = gain_far
    far = swap(far, "core")
    out_near, out_sent = step(
        lambda k, g: (k[:tok] + g[:tok].astype(f32), low(k[tok:] + g[tok:].astype(f32))),
        keep_o, out_got,
    )
    out_x = swap(out_sent, "x")
    for bit in bits[1:]:
        in_kept, in_got = z_step(in_kept, in_got, bit)
    rows_kept, rows_got = z_step(rows_kept, rows_got, bits[0])

    def own_grads(all_normed, grad_kv, grad_q):
        own = all_normed[:, :, :rows].reshape(group, features)
        grads = [dot_tn(own, grad_q), dot_tn(all_normed.reshape(-1, features), grad_kv)]
        return first_half(by_block(jnp.concatenate(grads, axis=1)), y_index)

    qkv_kept, qkv_sent = step(own_grads, normed_a, d_kv, d_query)
    qkv_got = swap(qkv_sent, "y")
    near, gain_near = back(0, after(d_kv_slots, turn_of[0]), f32)
    turn_of[0] = gain_near
    gains = jnp.concatenate([gain_far + gain_near, gain_f_part])
    gains_got = swap(gains, "core")

    def gain_step(exchange):
        summed = step(lambda k, g: k + g, gains, gains_got)
        return summed, exchange(summed)

    near, near_got = token_step(near, far, lambda v: swap(v, "x"))
    near, near_got = (v.reshape((z_count,) + v.shape[-3:]) for v in (near, near_got))
    output = step(lambda k, g: low(k + g.astype(f32)), out_near, out_x)
    output = output.reshape(2, rows, features)
    output_got = swap(output[1], "y")
    for bit in bits[1:]:
        rows_kept, rows_got = z_step(rows_kept, rows_got, bit)
    in_all = to_owners(total(in_kept, in_got))[None]
    qkv_kept, qkv_got = z_step(qkv_kept, qkv_got, bits[0])
    gains, gains_got = gain_step(lambda v: swap(v, "x"))
    for bit in reversed(bits[1:]):
        in_all = z_spread(in_all, bit)
    for bit in bits[1:]:
        qkv_kept, qkv_got = z_step(qkv_kept, qkv_got, bit)
    near, near_got = token_step(near, near_got, lambda v: swap_z(v, bits[0]))
    rows_all = total(rows_kept, rows_got)[None]
    gains, gains_got = gain_step(lambda v: swap(v, "y"))
    qkv_all = to_owners(total(qkv_kept, qkv_got))[None]
    for bit in bits[1:]:
        near, near_got = token_step(near, near_got, lambda v: swap_z(v, bit))
    in_all = z_spread(in_all, bits[0])
    in_y = swap(in_all, "y")
    for bit in reversed(bits[1:]):
        qkv_all = z_spread(qkv_all, bit)
        rows_all = z_spread(rows_all, bit)
    gains, gains_got = gain_step(lambda v: swap_z(v, bits[0]))
    near, near_got = after((near, near_got), turn_of[0])
    grad_tokens = finish(
        near.reshape(tok, features), near_got.reshape(tok, features), a_all, b_all,
        grad_middle, gain_a, rows,
    )
    grad_tokens = grad_tokens.reshape(2, rows, features)
    grad_got = swap(grad_tokens[1], "y")
    turn_of[0] = grad_tokens
    qkv_all = z_spread(qkv_all, bits[0])
    qkv_y = swap(qkv_all, "y")
    rows_all = z_spread(rows_all, bits[0])
    rows_y = swap(rows_all, "y")
    for bit in bits[1:]:
        gains, gains_got = gain_step(lambda v: swap_z(v, bit))
    gains = step(lambda k, g: k + g, gains, gains_got)
    output = pair_in_order(output[0], output_got, y_index)
    grad_tokens = pair_in_order(grad_tokens[0], grad_got, y_index)

    lead = w_rows // (2 * z_count)
    offsets = [reversed_bits(o) for o in z_offsets()]
    if lead % 8 == 0:

        def place_columns(own, got, parts):
            kernel = functools.partial(place_columns_kernel, parts, offsets)
            return place(kernel, index, own, got, [(w_rows, shards * own.shape[-1])])[0]

        d_out, d_attn = place(
            functools.partial(place_rows_kernel, offsets),
            index, rows_all, rows_y, [(ff, features), (w_rows, features)],
        )
    else:
        at_z = jnp.array(offsets) ^ index[2]
        chunk = jnp.concatenate([y_index * z_count + at_z, (1 - y_index) * z_count + at_z])
        ordered = lambda own, got: jnp.take(
            jnp.concatenate([own, got]), jnp.argsort(chunk), axis=0
        )

        def place_columns(own, got, parts):
            whole = jnp.take(ordered(own, got), slot_of, axis=1)
            whole = whole.reshape(2 * z_count, shards, lead, parts, -1).transpose(0, 2, 3, 1, 4)
            return whole.reshape(w_rows, -1).astype(f32)

        whole = ordered(rows_all, rows_y)
        d_out = whole[:, :out_lead].reshape(-1, features)[:ff].astype(f32)
        d_attn = whole[:, out_lead:].reshape(-1, features).astype(f32)

    return (
        output,
        grad_tokens,
        gains[0],
        gains[1],
        place_columns(qkv_all, qkv_y, 3),
        d_attn,
        place_columns(in_all, in_y, 2),
        d_out,
    )


def solution(mesh):
    shards, cycle = mesh.shape["shard"], mesh.shape["ctx"]
    fine = Mesh(mesh.devices.reshape(shards // 2, 2, cycle // 2, 2), ("x", "core", "z", "y"))
    by_token = P(None, ("z", "y", "x", "core"), None)
    by_row = P(("x", "core"), None)
    return jax.shard_map(
        local,
        mesh=fine,
        in_specs=(by_token, P(), P(), by_row, by_row, by_row, by_row, by_token),
        out_specs=(by_token, by_token, P(), P(), by_row, by_row, by_row, by_row),
        check_vma=False,
    )
```
